32 devices in a mesh: rep: 8 (over y, x, core), fsdp: 4 (over z).
Axes of the slice: x: 2, y: 2, z: 4, core: 2. Of those that a mesh axis runs over, the one named last changes fastest.
Arguments:
- tokens: bfloat16 [4096, 4096], P('rep', 'fsdp'), may hold values from -6 to 6
- gate_weight: bfloat16 [4096, 7168], P('rep', 'fsdp'), may hold values from -0.09375 to 0.09375
- up_act: bfloat16 [4096, 7168], P('rep', 'fsdp'), may hold values from -6 to 6
- cotangent: bfloat16 [4096, 7168], P('rep', 'fsdp'), may hold values from -0.099609375 to 0.099609375
Outputs:
- grad_sum: bfloat16 [4096, 7168], P('rep', 'fsdp')
- curvature: float32 [7168], P('fsdp')
- spread: float32 [7168], P('fsdp')
The draws below stay inside these ranges and needn't reach their ends.
All inputs are finite; a program needn't handle non-finite values.
Results may differ from the reference program's by a relative error of at most 0.024.
Values may be sent and summed in bfloat16 or wider, within the bound.
A program may use at most 128 MiB of HBM per device.

```python
import jax
import jax.numpy as jnp
from jax import lax

D = 4096
FF = 7168
TOK = 512
REPLICAS = 8
TOKENS = 4096


def shard_levels(rng, extent, cuts, smallest, largest):
    def one(dim, shards_of):
        heights = jax.random.uniform(jax.random.fold_in(jax.random.fold_in(rng, 6), dim), (shards_of,), jnp.float32, smallest / len(cuts), largest / len(cuts))
        return jnp.repeat(jnp.exp(heights), extent[dim] // shards_of).reshape((-1,) + (1,) * (len(extent) - dim - 1))

    loudness = one(*cuts[0])
    for cut in cuts[1:]:
        loudness = loudness * one(*cut)
    return loudness


def bell_draw(own_key, extent, spread, most, pieces=(), dtype=jnp.bfloat16):
    gain = shard_levels(own_key, extent, pieces, -0.22, 0.18) if pieces else 1.0
    entries = jax.random.normal(own_key, extent, jnp.float32) * spread * gain
    return jnp.minimum(jnp.maximum(entries, -most), most).astype(dtype)


def setup_inputs(seed: int = 0) -> dict:
    splits = jax.random.split(jax.random.key(seed), 5)
    return {
        "tokens": bell_draw(splits[0], (TOKENS, D), 1.0, 6.0, ((0, 8), (1, 4))),
        "gate_weight": bell_draw(splits[1], (D, FF), D ** -0.5, 0.09375, ((0, 8), (1, 4))),
        "up_act": bell_draw(splits[2], (TOKENS, FF), 1.0, 6.0, ((0, 8), (1, 4))),
        "cotangent": bell_draw(splits[3], (TOKENS, FF), 0.015625, 0.099609375, ((0, 8), (1, 4))),
    }


def local_terms(inputs, up_rows, cot_rows, gate_weight):
    gate_pre = jnp.dot(inputs, gate_weight, preferred_element_type=jnp.float32)
    sigmoid_gate = jax.nn.sigmoid(gate_pre)
    deriv_one = sigmoid_gate * (1.0 + gate_pre * (1.0 - sigmoid_gate))
    deriv_two = sigmoid_gate * (1.0 - sigmoid_gate) * (2.0 + gate_pre * (1.0 - 2.0 * sigmoid_gate))
    weighted = cot_rows.astype(jnp.float32) * up_rows.astype(jnp.float32)
    token_coeff = (weighted * deriv_one).astype(jnp.bfloat16)
    rep_grad = lax.dot_general(inputs, token_coeff, (((0,), (0,)), ((), ())), preferred_element_type=jnp.float32).astype(jnp.bfloat16)
    return rep_grad, weighted * deriv_two


def reference(tokens, gate_weight, up_act, cotangent):
    rows_in = tokens.reshape(REPLICAS, TOK, D)
    up_in = up_act.reshape(REPLICAS, TOK, FF)
    cot_in = cotangent.reshape(REPLICAS, TOK, FF)

    def first_pass(running, blocks):
        rep_grad, unused = local_terms(blocks[0], blocks[1], blocks[2], gate_weight)
        return running + rep_grad.astype(jnp.float32), None

    grad_acc, unused = lax.scan(first_pass, jnp.zeros((D, FF), jnp.float32), (rows_in, up_in, cot_in))
    grad_sum = grad_acc.astype(jnp.bfloat16)

    def second_pass(running, blocks):
        inputs = blocks[0]
        rep_grad, bend_weight = local_terms(inputs, blocks[1], blocks[2], gate_weight)
        own_proj = jnp.dot(inputs, rep_grad, preferred_element_type=jnp.float32)
        mean_proj = jnp.dot(inputs, grad_sum, preferred_element_type=jnp.float32) / REPLICAS
        deviate = own_proj - mean_proj
        curv_part = jnp.sum(bend_weight * mean_proj * mean_proj, axis=0)
        spread_part = jnp.sum(bend_weight * deviate * deviate, axis=0)
        return (running[0] + curv_part, running[1] + spread_part), None

    zeros_row = jnp.zeros((FF,), jnp.float32)
    sums, unused = lax.scan(second_pass, (zeros_row, zeros_row), (rows_in, up_in, cot_in))
    return grad_sum, sums[0], sums[1] / (REPLICAS - 1)
```

```python
import functools

import jax
import jax.numpy as jnp
from jax import lax
from jax.experimental import pallas as pl
from jax.experimental.pallas import tpu as pltpu
from jax.sharding import PartitionSpec as P

MESH = pl.DeviceIdType.MESH
ANY = pl.BlockSpec(memory_space=pl.ANY)


def rep_bits(r):
    return r // 4, (r // 2) % 2, r % 2


def flip(r, m):
    y, x, c = rep_bits(r)
    y = 1 - y if m & 4 else y
    x = 1 - x if m & 2 else x
    c = 1 - c if m & 1 else c
    return y * 4 + x * 2 + c


def when(cond, fn):
    if cond is True:
        fn()
    else:
        pl.when(cond)(fn)


def both(a, b):
    if a is True:
        return b
    if b is True:
        return a
    return jnp.logical_and(a, b)


def greet(zs, r, z, masks, reach):
    barrier = pltpu.get_barrier_semaphore()
    for m in masks:
        pl.semaphore_signal(barrier, inc=1, device_id=(flip(r, m), z), device_id_type=MESH)
    if not reach:
        pl.semaphore_wait(barrier, len(masks))
        return

    @pl.when(z > 0)
    def _():
        pl.semaphore_signal(barrier, inc=1, device_id=(r, z - 1), device_id_type=MESH)

    @pl.when(z < zs - 1)
    def _():
        pl.semaphore_signal(barrier, inc=1, device_id=(r, z + 1), device_id_type=MESH)

    edge = jnp.where(z > 0, 1, 0) + jnp.where(z < zs - 1, 1, 0)
    pl.semaphore_wait(barrier, len(masks) + edge)


def gather_kernel(zs, nr, t_ref, w_ref, u_ref, ta, wa, ua, tv, wv, uv, s_x, s_y, s_u, s_d, s_c, r_t, r_c, s_a, r_a, s_l):
    r, z = lax.axis_index("rep"), lax.axis_index("fsdp")
    rows, feats = t_ref.shape
    part = rows // 4
    greet(zs, r, z, range(1, nr), True)
    pending = []

    def region(ref, m, q, zo):
        return ref.at[
            pl.ds(pl.multiple_of(flip(r, m) * rows + q * part, part), part),
            pl.ds(pl.multiple_of(zo * feats, feats), feats),
        ]

    def rsem(m, q, zo):
        return ((m // 2) * 4 + q) * zs + zo

    def push(cond, m, q, zo, way, slot):
        own = m == 0 and zo is z
        src = t_ref.at[pl.ds(q * part, part), :] if own else region(ta, m, q, zo)
        dst = region(ta, m, q, zo)
        if way == "x":
            to, sem, kind, rs = (flip(r, 2), z), s_x, m ^ 2, r_t
        elif way == "y":
            to, sem, kind, rs = (flip(r, 4), z), s_y, m ^ 4, r_t
        elif way == "u":
            to, sem, kind, rs = (r, z + 1), s_u, m, r_t
        elif way == "d":
            to, sem, kind, rs = (r, z - 1), s_d, m, r_t
        else:
            to, sem, kind, rs = (flip(r, 1), z), s_c, m, r_c
        copy = pltpu.make_async_remote_copy(
            src_ref=src, dst_ref=dst, send_sem=sem.at[slot], recv_sem=rs.at[rsem(kind, q, zo)],
            device_id=to, device_id_type=MESH,
        )
        when(cond, copy.start)
        pending.append((cond, copy))

    def xy_slot(q, zo, relay):
        base = 3 if q >= 2 else 0
        return base + (zo * 3 if q >= 2 else 0) + (2 if relay else q % 2)

    def z_slot(m, q, zo):
        return (((m // 2) * 2 + q) if q < 2 else 8 + q - 2) * zs + zo

    def go_up(cond, m, q, zo):
        push(both(cond, z < zs - 1), m, q, zo, "u", z_slot(m, q, zo))

    def go_down(cond, m, q, zo):
        push(both(cond, z > 0), m, q, zo, "d", z_slot(m, q, zo))

    def go_xy(cond, q, zo):
        push(cond, 0, q, zo, "x", xy_slot(q, zo, False))
        push(cond, 0, q, zo, "y", xy_slot(q, zo, False))

    def go_core(cond, m, q, zo):
        push(cond, m, q, zo, "c", rsem(m, q, zo))

    keep = pltpu.make_async_copy(t_ref, tv, s_l.at[0])
    keep_w = pltpu.make_async_copy(w_ref.at[r], wv, s_l.at[1])
    keep_u = pltpu.make_async_copy(u_ref.at[r], uv, s_l.at[2])
    for copy in (keep, keep_w, keep_u):
        copy.start()
    for q in (0, 1):
        go_xy(True, q, z)
    for q in (2, 3, 0, 1):
        go_up(True, 0, q, z)
        go_down(True, 0, q, z)
    swaps = []
    for a, (src, dst) in enumerate(((w_ref, wa), (u_ref, ua))):
        for m in range(1, nr):
            copy = pltpu.make_async_remote_copy(
                src_ref=src.at[flip(r, m)], dst_ref=dst.at[r],
                send_sem=s_a.at[a, m], recv_sem=r_a.at[a, m],
                device_id=(flip(r, m), z), device_id_type=MESH,
            )
            swaps.append(copy)
    for copy in swaps[: nr - 1]:
        copy.start()
    for q in (2, 3):
        go_xy(True, q, z)
    for copy in swaps[nr - 1 :]:
        copy.start()
    for q in range(4):
        go_core(True, 0, q, z)
    for copy in (keep, keep_w, keep_u):
        copy.wait()
    mine = ta.at[
        pl.ds(pl.multiple_of(r * rows, rows), rows), pl.ds(pl.multiple_of(z * feats, feats), feats)
    ]
    keep = pltpu.make_async_copy(tv, mine, s_l.at[0])
    keep_w = pltpu.make_async_copy(wv, wa.at[r], s_l.at[1])
    keep_u = pltpu.make_async_copy(uv, ua.at[r], s_l.at[2])
    for copy in (keep, keep_w, keep_u):
        copy.start()

    items = []
    hops = {0: 0, 2: 1, 4: 1, 6: 2}
    for m in (0, 2, 4, 6):
        for d in range(-(zs - 1), zs):
            if m == 0 and d == 0:
                continue
            for q in range(4):
                items.append((hops[m] + abs(d), m if d == 0 or q >= 2 else m, q, d))
    items.sort(key=lambda i: (i[0], abs(i[3])))
    for _, m, q, d in items:
        zo = z if d == 0 else z + d
        valid = True if d == 0 else (zo >= 0 if d < 0 else zo < zs)
        got = pltpu.make_async_copy(region(ta, m, q, zo), region(ta, m, q, zo), r_t.at[rsem(m, q, zo)])
        when(valid, got.wait)
        if q < 2:
            if d == 0:
                if m == 4 and q == 0:
                    push(True, 4, 0, z, "x", xy_slot(0, z, True))
                if m == 2 and q == 1:
                    push(True, 2, 1, z, "y", xy_slot(1, z, True))
                go_up(True, m, q, z)
                go_down(True, m, q, z)
            elif d < 0:
                go_up(valid, m, q, zo)
            else:
                go_down(valid, m, q, zo)
        else:
            if m == 0:
                go_xy(valid, q, zo)
                if d < 0:
                    go_up(valid, 0, q, zo)
                else:
                    go_down(valid, 0, q, zo)
            if m == 4 and q == 2:
                push(valid, 4, 2, zo, "x", xy_slot(2, zo, True))
            if m == 2 and q == 3:
                push(valid, 2, 3, zo, "y", xy_slot(3, zo, True))
        go_core(valid, m, q, zo)
    for copy in (keep, keep_w, keep_u):
        copy.wait()
    for copy in swaps:
        copy.wait()
    for cond, copy in pending:
        when(cond, copy.wait_send)
    for m in (0, 2, 4, 6):
        for q in range(4):
            for zo in range(zs):
                spot = region(ta, m | 1, q, zo)
                pltpu.make_async_copy(spot, spot, r_c.at[rsem(m, q, zo)]).wait()


def gather_all(zs, nr, tokens, w, u):
    rows, feats = tokens.shape
    dma = pltpu.SemaphoreType.DMA
    full = zs * 16
    return pl.pallas_call(
        functools.partial(gather_kernel, zs, nr),
        out_shape=(
            jax.ShapeDtypeStruct((rows * nr, feats * zs), tokens.dtype),
            jax.ShapeDtypeStruct(w.shape, w.dtype),
            jax.ShapeDtypeStruct(u.shape, u.dtype),
        ),
        in_specs=[ANY] * 3,
        out_specs=(ANY,) * 3,
        scratch_shapes=[
            pltpu.VMEM(tokens.shape, tokens.dtype),
            pltpu.VMEM(w.shape[1:], w.dtype),
            pltpu.VMEM(u.shape[1:], u.dtype),
            dma((3 + 3 * zs,)), dma((3 + 3 * zs,)), dma((10 * zs,)), dma((10 * zs,)), dma((full,)),
            dma((full,)), dma((full,)), dma((2, nr)), dma((2, nr)), dma((3,)),
        ],
        compiler_params=pltpu.CompilerParams(collective_id=0, has_side_effects=True),
    )(tokens, w, u)


def return_kernel(nr, g_ref, p_ref, ga, pa, gv, pv, s_a, r_a, s_l):
    r, z = lax.axis_index("rep"), lax.axis_index("fsdp")
    greet(0, r, z, range(1, nr), False)
    swaps = []
    for m in range(1, nr):
        there = flip(r, m)
        for a, (src, dst) in enumerate(((g_ref.at[there], ga.at[r]), (p_ref, pa.at[r]))):
            copy = pltpu.make_async_remote_copy(
                src_ref=src, dst_ref=dst, send_sem=s_a.at[a, m], recv_sem=r_a.at[a, m],
                device_id=(there, z), device_id_type=MESH,
            )
            copy.start()
            swaps.append(copy)
    for src, mid, dst, a in ((g_ref.at[r], gv, ga.at[r], 0), (p_ref, pv, pa.at[r], 1)):
        copy = pltpu.make_async_copy(src, mid, s_l.at[a])
        copy.start()
        copy.wait()
        copy = pltpu.make_async_copy(mid, dst, s_l.at[a])
        copy.start()
        copy.wait()
    for copy in swaps:
        copy.wait()


def give_back(nr, grads, parts):
    dma = pltpu.SemaphoreType.DMA
    return pl.pallas_call(
        functools.partial(return_kernel, nr),
        out_shape=(
            jax.ShapeDtypeStruct(grads.shape, grads.dtype),
            jax.ShapeDtypeStruct((nr,) + parts.shape, parts.dtype),
        ),
        in_specs=[ANY] * 2,
        out_specs=(ANY,) * 2,
        scratch_shapes=[
            pltpu.VMEM(grads.shape[1:], grads.dtype),
            pltpu.VMEM(parts.shape, parts.dtype),
            dma((2, nr)), dma((2, nr)), dma((2,)),
        ],
        compiler_params=pltpu.CompilerParams(collective_id=1, has_side_effects=True),
    )(grads, parts)


def derivatives(gate_pre):
    s = jax.nn.sigmoid(gate_pre)
    one = s * (1.0 + gate_pre * (1.0 - s))
    two = s * (1.0 - s) * (2.0 + gate_pre * (1.0 - 2.0 * s))
    return one, two


def units_split(zs, nr, tokens, gate_weight, up_act, cotangent):
    rows, _ = tokens.shape
    hidden = gate_weight.shape[1]
    cols = hidden // nr

    def by_unit(a):
        return a.reshape(a.shape[0], nr, cols).transpose(1, 0, 2)

    product = cotangent.astype(jnp.float32) * up_act.astype(jnp.float32)
    t_all, w_all, u_all = gather_all(
        zs, nr, tokens, by_unit(gate_weight), by_unit(product.astype(jnp.bfloat16))
    )
    model = t_all.shape[1]
    gate_pre = jnp.dot(t_all, w_all.reshape(model, cols), preferred_element_type=jnp.float32)
    one, two = derivatives(gate_pre)
    weighted = u_all.reshape(nr * rows, cols).astype(jnp.float32)
    coeff = (weighted * one).astype(jnp.bfloat16).reshape(nr, rows, cols)
    bend = weighted * two
    t_rep = t_all.reshape(nr, rows, model)
    rep_grad = lax.dot_general(
        t_rep, coeff, (((1,), (1,)), ((0,), (0,))), preferred_element_type=jnp.float32
    ).astype(jnp.bfloat16)
    own = lax.dot_general(
        t_rep, rep_grad, (((2,), (1,)), ((0,), (0,))), preferred_element_type=jnp.float32
    ).reshape(nr * rows, cols)
    grad_sum = jnp.sum(rep_grad.astype(jnp.float32), axis=0).astype(jnp.bfloat16)
    mean = jnp.dot(t_all, grad_sum, preferred_element_type=jnp.float32) / nr
    dev = own - mean
    curv = jnp.sum(bend * mean * mean, axis=0)
    spread = jnp.sum(bend * dev * dev, axis=0) / (nr - 1)
    parts = jnp.pad(jnp.stack([curv, spread]), ((0, 6), (0, -cols % 128)))
    g_all, p_all = give_back(nr, grad_sum.reshape(nr, model // nr, cols), parts)
    grad_rows = g_all.transpose(1, 0, 2).reshape(model // nr, hidden)
    stats = p_all[:, :, :cols]
    return grad_rows, stats[:, 0].reshape(hidden), stats[:, 1].reshape(hidden)


def tokens_split(tokens, gate_weight, up_act, cotangent):
    features_all = lax.all_gather(tokens, "fsdp", axis=1, tiled=True)
    replicas = lax.axis_size("rep")

    def add_rows(block_rows):
        return jnp.dot(features_all, block_rows, preferred_element_type=jnp.float32)

    one, two = derivatives(add_rows(lax.all_gather(gate_weight, "rep", axis=0, tiled=True)))
    weighted = cotangent.astype(jnp.float32) * up_act.astype(jnp.float32)
    coeff = (weighted * one).astype(jnp.bfloat16)
    bend = weighted * two
    rep_grad = lax.dot_general(
        features_all, coeff, (((0,), (0,)), ((), ())), preferred_element_type=jnp.float32
    ).astype(jnp.bfloat16)
    own_proj = jnp.dot(features_all, rep_grad, preferred_element_type=jnp.float32)
    grad_shard = lax.psum_scatter(rep_grad, "rep", scatter_dimension=0, tiled=True)
    mean_proj = add_rows(lax.all_gather(grad_shard, "rep", axis=0, tiled=True)) / replicas
    dev = own_proj - mean_proj
    curv_part = jnp.sum(bend * mean_proj * mean_proj, axis=0)
    spread_part = jnp.sum(bend * dev * dev, axis=0)
    curvature, spread = lax.psum((curv_part, spread_part), "rep")
    return grad_shard, curvature, spread / (replicas - 1)


def solution(mesh):
    zs, nr = mesh.shape["fsdp"], mesh.shape["rep"]
    body = functools.partial(units_split, zs, nr) if nr == 8 and zs <= 4 else tokens_split
    placed = (P("rep", "fsdp"),) * 4
    return jax.shard_map(
        body,
        mesh=mesh,
        in_specs=placed,
        out_specs=(P("rep", "fsdp"), P("fsdp"), P("fsdp")),
        check_vma=False,
    )
```

```python
import functools

import jax
import jax.numpy as jnp
from jax import lax
from jax.experimental import pallas as pl
from jax.experimental.pallas import tpu as pltpu
from jax.sharding import PartitionSpec as P

MESH = pl.DeviceIdType.MESH
ANY = pl.BlockSpec(memory_space=pl.ANY)


def rep_bits(r):
    return r // 4, (r // 2) % 2, r % 2


def flip(r, m):
    y, x, c = rep_bits(r)
    y = 1 - y if m & 4 else y
    x = 1 - x if m & 2 else x
    c = 1 - c if m & 1 else c
    return y * 4 + x * 2 + c


def when(cond, fn):
    if cond is True:
        fn()
    else:
        pl.when(cond)(fn)


def both(a, b):
    if a is True:
        return b
    if b is True:
        return a
    return jnp.logical_and(a, b)


def span(ref, k):
    size = ref.shape[1] // 8
    return ref.at[:, pl.ds(pl.multiple_of(k * size, size), size)]


def greet(zs, r, z, masks, reach):
    barrier = pltpu.get_barrier_semaphore()
    for m in masks:
        pl.semaphore_signal(barrier, inc=1, device_id=(flip(r, m), z), device_id_type=MESH)
    if not reach:
        pl.semaphore_wait(barrier, len(masks))
        return

    @pl.when(z > 0)
    def _():
        pl.semaphore_signal(barrier, inc=1, device_id=(r, z - 1), device_id_type=MESH)

    @pl.when(z < zs - 1)
    def _():
        pl.semaphore_signal(barrier, inc=1, device_id=(r, z + 1), device_id_type=MESH)

    edge = jnp.where(z > 0, 1, 0) + jnp.where(z < zs - 1, 1, 0)
    pl.semaphore_wait(barrier, len(masks) + edge)


def gather_kernel(zs, nr, t_ref, w_ref, u_ref, ta, wa, ua, tv, wv, uv, s_x, s_y, s_u, s_d, s_c, r_t, r_c, s_a, r_a, s_l):
    r, z = lax.axis_index("rep"), lax.axis_index("fsdp")
    rows, feats = t_ref.shape
    part = rows // 4
    greet(zs, r, z, range(1, nr), True)
    pending = []

    def region(ref, m, q, zo):
        return ref.at[
            pl.ds(pl.multiple_of(flip(r, m) * rows + q * part, part), part),
            pl.ds(pl.multiple_of(zo * feats, feats), feats),
        ]

    def rsem(m, q, zo):
        return ((m // 2) * 4 + q) * zs + zo

    def push(cond, m, q, zo, way, slot):
        own = m == 0 and zo is z
        src = t_ref.at[pl.ds(q * part, part), :] if own else region(ta, m, q, zo)
        dst = region(ta, m, q, zo)
        if way == "x":
            to, sem, kind, rs = (flip(r, 2), z), s_x, m ^ 2, r_t
        elif way == "y":
            to, sem, kind, rs = (flip(r, 4), z), s_y, m ^ 4, r_t
        elif way == "u":
            to, sem, kind, rs = (r, z + 1), s_u, m, r_t
        elif way == "d":
            to, sem, kind, rs = (r, z - 1), s_d, m, r_t
        else:
            to, sem, kind, rs = (flip(r, 1), z), s_c, m, r_c
        copy = pltpu.make_async_remote_copy(
            src_ref=src, dst_ref=dst, send_sem=sem.at[slot], recv_sem=rs.at[rsem(kind, q, zo)],
            device_id=to, device_id_type=MESH,
        )
        when(cond, copy.start)
        pending.append((cond, copy))

    def xy_slot(q, zo, relay):
        base = 3 if q >= 2 else 0
        return base + (zo * 3 if q >= 2 else 0) + (2 if relay else q % 2)

    def z_slot(m, q, zo):
        return (((m // 2) * 2 + q) if q < 2 else 8 + q - 2) * zs + zo

    def go_up(cond, m, q, zo):
        push(both(cond, z < zs - 1), m, q, zo, "u", z_slot(m, q, zo))

    def go_down(cond, m, q, zo):
        push(both(cond, z > 0), m, q, zo, "d", z_slot(m, q, zo))

    def go_xy(cond, q, zo):
        push(cond, 0, q, zo, "x", xy_slot(q, zo, False))
        push(cond, 0, q, zo, "y", xy_slot(q, zo, False))

    def go_core(cond, m, q, zo):
        push(cond, m, q, zo, "c", rsem(m, q, zo))

    keep = pltpu.make_async_copy(t_ref, tv, s_l.at[0])
    keep_w = pltpu.make_async_copy(w_ref.at[r], wv, s_l.at[1])
    keep_u = pltpu.make_async_copy(u_ref.at[r], uv, s_l.at[2])
    for copy in (keep, keep_w, keep_u):
        copy.start()
    for q in (0, 1):
        go_xy(True, q, z)
    for q in (2, 3, 0, 1):
        go_up(True, 0, q, z)
        go_down(True, 0, q, z)
    swaps = []
    for a, (src, dst) in enumerate(((w_ref, wa), (u_ref, ua))):
        for m in range(1, nr):
            copy = pltpu.make_async_remote_copy(
                src_ref=src.at[flip(r, m)], dst_ref=span(dst, r),
                send_sem=s_a.at[a, m], recv_sem=r_a.at[a, m],
                device_id=(flip(r, m), z), device_id_type=MESH,
            )
            swaps.append(copy)
    for copy in swaps[: nr - 1]:
        copy.start()
    for q in (2, 3):
        go_xy(True, q, z)
    for q in range(4):
        go_core(True, 0, q, z)
    for copy in (keep, keep_w, keep_u):
        copy.wait()
    mine = ta.at[
        pl.ds(pl.multiple_of(r * rows, rows), rows), pl.ds(pl.multiple_of(z * feats, feats), feats)
    ]
    keep = pltpu.make_async_copy(tv, mine, s_l.at[0])
    keep_w = pltpu.make_async_copy(wv, span(wa, r), s_l.at[1])
    keep_u = pltpu.make_async_copy(uv, span(ua, r), s_l.at[2])
    for copy in (keep, keep_w, keep_u):
        copy.start()

    items = []
    hops = {0: 0, 2: 1, 4: 1, 6: 2}
    for m in (0, 2, 4, 6):
        for d in range(-(zs - 1), zs):
            if m == 0 and d == 0:
                continue
            for q in range(4):
                items.append((hops[m] + abs(d), m if d == 0 or q >= 2 else m, q, d))
    items.sort(key=lambda i: (i[0], abs(i[3])))
    late = swaps[nr - 1 :]
    for turn, m, q, d in items:
        if turn > 2 and late:
            for copy in late:
                copy.start()
            late = []
        zo = z if d == 0 else z + d
        valid = True if d == 0 else (zo >= 0 if d < 0 else zo < zs)
        got = pltpu.make_async_copy(region(ta, m, q, zo), region(ta, m, q, zo), r_t.at[rsem(m, q, zo)])
        when(valid, got.wait)
        if q < 2:
            if d == 0:
                if m == 4 and q == 0:
                    push(True, 4, 0, z, "x", xy_slot(0, z, True))
                if m == 2 and q == 1:
                    push(True, 2, 1, z, "y", xy_slot(1, z, True))
                go_up(True, m, q, z)
                go_down(True, m, q, z)
            elif d < 0:
                go_up(valid, m, q, zo)
            else:
                go_down(valid, m, q, zo)
        else:
            if m == 0:
                go_xy(valid, q, zo)
                if d < 0:
                    go_up(valid, 0, q, zo)
                else:
                    go_down(valid, 0, q, zo)
            if m == 4 and q == 2:
                push(valid, 4, 2, zo, "x", xy_slot(2, zo, True))
            if m == 2 and q == 3:
                push(valid, 2, 3, zo, "y", xy_slot(3, zo, True))
        go_core(valid, m, q, zo)
    for copy in (keep, keep_w, keep_u):
        copy.wait()
    for copy in swaps:
        copy.wait()
    for cond, copy in pending:
        when(cond, copy.wait_send)
    for m in (0, 2, 4, 6):
        for q in range(4):
            for zo in range(zs):
                spot = region(ta, m | 1, q, zo)
                pltpu.make_async_copy(spot, spot, r_c.at[rsem(m, q, zo)]).wait()


def gather_all(zs, nr, tokens, w, u):
    rows, feats = tokens.shape
    dma = pltpu.SemaphoreType.DMA
    full = zs * 16
    return pl.pallas_call(
        functools.partial(gather_kernel, zs, nr),
        out_shape=(
            jax.ShapeDtypeStruct((rows * nr, feats * zs), tokens.dtype),
            jax.ShapeDtypeStruct((w.shape[1], nr * w.shape[2]), w.dtype),
            jax.ShapeDtypeStruct((u.shape[1], nr * u.shape[2]), u.dtype),
        ),
        in_specs=[ANY] * 3,
        out_specs=(ANY,) * 3,
        scratch_shapes=[
            pltpu.VMEM(tokens.shape, tokens.dtype),
            pltpu.VMEM(w.shape[1:], w.dtype),
            pltpu.VMEM(u.shape[1:], u.dtype),
            dma((3 + 3 * zs,)), dma((3 + 3 * zs,)), dma((10 * zs,)), dma((10 * zs,)), dma((full,)),
            dma((full,)), dma((full,)), dma((2, nr)), dma((2, nr)), dma((3,)),
        ],
        compiler_params=pltpu.CompilerParams(collective_id=0, has_side_effects=True),
    )(tokens, w, u)


def return_kernel(nr, g_ref, p_ref, ga, pa, gv, pv, s_a, r_a, s_l):
    r, z = lax.axis_index("rep"), lax.axis_index("fsdp")
    greet(0, r, z, range(1, nr), False)
    swaps = []
    for m in range(1, nr):
        there = flip(r, m)
        for a, (src, dst) in enumerate(((span(g_ref, there), ga.at[r]), (p_ref, pa.at[r]))):
            copy = pltpu.make_async_remote_copy(
                src_ref=src, dst_ref=dst, send_sem=s_a.at[a, m], recv_sem=r_a.at[a, m],
                device_id=(there, z), device_id_type=MESH,
            )
            copy.start()
            swaps.append(copy)
    for src, mid, dst, a in ((span(g_ref, r), gv, ga.at[r], 0), (p_ref, pv, pa.at[r], 1)):
        copy = pltpu.make_async_copy(src, mid, s_l.at[a])
        copy.start()
        copy.wait()
        copy = pltpu.make_async_copy(mid, dst, s_l.at[a])
        copy.start()
        copy.wait()
    for copy in swaps:
        copy.wait()


def give_back(nr, grads, parts):
    dma = pltpu.SemaphoreType.DMA
    return pl.pallas_call(
        functools.partial(return_kernel, nr),
        out_shape=(
            jax.ShapeDtypeStruct((nr, grads.shape[0], grads.shape[1] // nr), grads.dtype),
            jax.ShapeDtypeStruct((nr,) + parts.shape, parts.dtype),
        ),
        in_specs=[ANY] * 2,
        out_specs=(ANY,) * 2,
        scratch_shapes=[
            pltpu.VMEM((grads.shape[0], grads.shape[1] // nr), grads.dtype),
            pltpu.VMEM(parts.shape, parts.dtype),
            dma((2, nr)), dma((2, nr)), dma((2,)),
        ],
        compiler_params=pltpu.CompilerParams(collective_id=1, has_side_effects=True),
    )(grads, parts)


def derivatives(gate_pre):
    s = jax.nn.sigmoid(gate_pre)
    one = s * (1.0 + gate_pre * (1.0 - s))
    two = s * (1.0 - s) * (2.0 + gate_pre * (1.0 - 2.0 * s))
    return one, two


def units_split(zs, nr, tokens, gate_weight, up_act, cotangent):
    rows, _ = tokens.shape
    hidden = gate_weight.shape[1]
    cols = hidden // nr

    def by_unit(a):
        return a.T.reshape(nr, cols, a.shape[0])

    product = cotangent.astype(jnp.float32) * up_act.astype(jnp.float32)
    t_all, w_all, u_all = gather_all(
        zs, nr, tokens, by_unit(gate_weight), by_unit(product.astype(jnp.bfloat16))
    )
    model = t_all.shape[1]

    def project(left, block):
        return lax.dot_general(left, block, (((1,), (1,)), ((), ())), preferred_element_type=jnp.float32)

    one, two = derivatives(project(w_all, t_all))
    weighted = u_all.astype(jnp.float32)
    coeff = (weighted * one).astype(jnp.bfloat16)
    bend = weighted * two
    grad_acc, rep_grads = 0.0, []
    for k in range(nr):
        block = t_all[k * rows : (k + 1) * rows]
        rep_grad = jnp.dot(
            coeff[:, k * rows : (k + 1) * rows], block, preferred_element_type=jnp.float32
        ).astype(jnp.bfloat16)
        rep_grads.append(rep_grad)
        grad_acc = grad_acc + rep_grad.astype(jnp.float32)
    grad_sum = grad_acc.astype(jnp.bfloat16)
    mean = project(grad_sum, t_all) / nr
    curv = jnp.sum(bend * mean * mean, axis=1)
    spread = 0.0
    for k in range(nr):
        part = slice(k * rows, (k + 1) * rows)
        dev = project(rep_grads[k], t_all[part]) - mean[:, part]
        spread = spread + jnp.sum(bend[:, part] * dev * dev, axis=1)
    spread = spread / (nr - 1)
    parts = jnp.pad(jnp.stack([curv, spread]), ((0, 6), (0, -cols % 128)))
    g_all, p_all = give_back(nr, grad_sum, parts)
    grad_rows = g_all.reshape(hidden, model // nr).T
    stats = p_all[:, :, :cols]
    return grad_rows, stats[:, 0].reshape(hidden), stats[:, 1].reshape(hidden)


def tokens_split(tokens, gate_weight, up_act, cotangent):
    features_all = lax.all_gather(tokens, "fsdp", axis=1, tiled=True)
    replicas = lax.axis_size("rep")

    def add_rows(block_rows):
        return jnp.dot(features_all, block_rows, preferred_element_type=jnp.float32)

    one, two = derivatives(add_rows(lax.all_gather(gate_weight, "rep", axis=0, tiled=True)))
    weighted = cotangent.astype(jnp.float32) * up_act.astype(jnp.float32)
    coeff = (weighted * one).astype(jnp.bfloat16)
    bend = weighted * two
    rep_grad = lax.dot_general(
        features_all, coeff, (((0,), (0,)), ((), ())), preferred_element_type=jnp.float32
    ).astype(jnp.bfloat16)
    own_proj = jnp.dot(features_all, rep_grad, preferred_element_type=jnp.float32)
    grad_shard = lax.psum_scatter(rep_grad, "rep", scatter_dimension=0, tiled=True)
    mean_proj = add_rows(lax.all_gather(grad_shard, "rep", axis=0, tiled=True)) / replicas
    dev = own_proj - mean_proj
    curv_part = jnp.sum(bend * mean_proj * mean_proj, axis=0)
    spread_part = jnp.sum(bend * dev * dev, axis=0)
    curvature, spread = lax.psum((curv_part, spread_part), "rep")
    return grad_shard, curvature, spread / (replicas - 1)


def solution(mesh):
    zs, nr = mesh.shape["fsdp"], mesh.shape["rep"]
    body = functools.partial(units_split, zs, nr) if nr == 8 and zs <= 4 else tokens_split
    placed = (P("rep", "fsdp"),) * 4
    return jax.shard_map(
        body,
        mesh=mesh,
        in_specs=placed,
        out_specs=(P("rep", "fsdp"), P("fsdp"), P("fsdp")),
        check_vma=False,
    )
```
